32 devices in a mesh: row: 4 (over y, x), col: 8 (over z, core).
Axes of the slice: x: 2, y: 2, z: 4, core: 2. Of those that a mesh axis runs over, the one named last changes fastest.
Arguments:
- b_steps: float32 [2, 1024, 2048], P(None, 'row', 'col'), may hold values from -6 to 6
- b_trail: float32 [4096, 2048], P('row', 'col'), may hold values from -6 to 6
- l_cross: float32 [1024, 1024], P('row', 'col'), may hold values from -0.1875 to 0.1875
- l_trail: float32 [2, 4096, 1024], P(None, 'row', 'col'), may hold values from -0.125 to 0.125
- diag_inv: float32 [2, 2, 512, 512], P(None, None, None, 'col'), may hold values from -1.5 to 1.5, as said below
- diag_low: float32 [2, 512, 512], P(None, None, 'col'), may hold values from -0.25 to 0.25
Outputs:
- x_steps: float32 [2, 1024, 2048], P(None, 'row', 'col')
- trail_out: float32 [4096, 2048], P('row', 'col')
The draws below stay inside these ranges and needn't reach their ends.
Inputs may be any that keep to these rules, and one draw needn't show every extreme that they name: Each diag_inv[s, h] is lower triangular with diagonal entries of 0.5 to 1.5 and strictly lower entries of magnitude at most 3 / sqrt(512).
All inputs are finite; a program needn't handle non-finite values.
Results may differ from the reference program's by a relative error of at most 0.00013.
Values sent between devices are 32-bit elements; how exact they have to be, the bound alone decides.
No kernel may reach another device: no remote copies, remote signals or barrier semaphores. Data moves between devices by JAX's collectives and lax.ppermute only.
A program may use at most 64 MiB of HBM per device.

```python
import math
import jax
import jax.numpy as jnp
from jax import lax

NB = 1024
H = 512
RHS = 2048
TRAIL = 4096


def draw_diag_inv(key, part):
    key_strict = jax.random.fold_in(key, 11)
    key_diagonal = jax.random.fold_in(key, 23)
    array_dims = (2, 2, H, H)
    strict = jnp.clip(jax.random.normal(key_strict, array_dims, jnp.float32), -3.0, 3.0) / math.sqrt(H)
    diagonal = jax.random.uniform(key_diagonal, (2, 2, H), jnp.float32, 0.5, 1.5)
    lower = jnp.tril(strict, -1) + diagonal[..., None] * jnp.eye(H, dtype=jnp.float32)
    return lower.astype(jnp.float32)


def levels(key, shape, split, least, largest):
    def one(axis_at, parts):
        draws = jax.random.uniform(jax.random.fold_in(jax.random.fold_in(key, 6), axis_at), (parts,), jnp.float32, least / len(split), largest / len(split))
        return jnp.repeat(jnp.exp(draws), shape[axis_at] // parts).reshape((-1,) + (1,) * (len(shape) - axis_at - 1))

    loudness = one(*split[0])
    for cut in split[1:]:
        loudness = loudness * one(*cut)
    return loudness


def normal_values(rng, extent, scale, limit, shards=(), kind=jnp.bfloat16):
    array = scale * jax.random.normal(rng, extent, jnp.float32)
    if shards:
        array = array * levels(rng, extent, shards, -0.22, 0.18)
    return jnp.clip(array, -limit, limit).astype(kind)


def setup_inputs(seed: int = 0) -> dict:
    splits = jax.random.split(jax.random.key(seed), 7)
    return {
        "b_steps": normal_values(splits[0], (2, NB, RHS), 1.0, 6.0, ((1, 4), (2, 8)), jnp.float32),
        "b_trail": normal_values(splits[1], (TRAIL, RHS), 1.0, 6.0, ((0, 4), (1, 8)), jnp.float32),
        "l_cross": normal_values(splits[2], (NB, NB), NB ** -0.5, 0.1875, ((0, 4), (1, 8)), jnp.float32),
        "l_trail": normal_values(splits[3], (2, TRAIL, NB), (2 * NB) ** -0.5, 0.125, ((1, 4), (2, 8)), jnp.float32),
        "diag_inv": draw_diag_inv(jax.random.fold_in(splits[6], 71), 0),
        "diag_low": normal_values(splits[5], (2, H, H), H ** -0.5, 0.25, ((2, 8),), jnp.float32),
    }


exact_prec = lax.Precision.HIGHEST


def mult(left_mat, right_mat):
    return jnp.dot(left_mat, right_mat, precision=exact_prec, preferred_element_type=jnp.float32)


def joined_inverse(inv_pair, low_block):
    inv_first = inv_pair[0]
    inv_second = inv_pair[1]
    lower_left = -mult(inv_second, mult(low_block, inv_first))
    upper = jnp.concatenate([inv_first, jnp.zeros_like(inv_first)], 1)
    bottom = jnp.concatenate([lower_left, inv_second], 1)
    return jnp.concatenate([upper, bottom], 0)


def reference(b_steps, b_trail, l_cross, l_trail, diag_inv, diag_low):
    joined_first = joined_inverse(diag_inv[0], diag_low[0])
    solved_first = mult(joined_first, b_steps[0])
    next_rows = b_steps[1] - mult(l_cross, solved_first)
    trail_mid = b_trail - mult(l_trail[0], solved_first)
    joined_second = joined_inverse(diag_inv[1], diag_low[1])
    solved_second = mult(joined_second, next_rows)
    trail_out = trail_mid - mult(l_trail[1], solved_second)
    return jnp.stack([solved_first, solved_second]), trail_out
```

```python
import functools

import jax
import jax.numpy as jnp
from jax import lax
from jax.experimental import pallas as pl
from jax.experimental.pallas import tpu as pltpu
from jax.sharding import PartitionSpec as P


exact_prec = lax.Precision.HIGHEST
LANES = 128
f32 = jnp.float32
bf16 = jnp.bfloat16


def mult(left_mat, right_mat):
    return jnp.dot(left_mat, right_mat, precision=exact_prec, preferred_element_type=f32)


def inverse_columns(diag_inv, diag_low, section, offset, own_rows):
    inv_first = diag_inv[section, 0]
    inv_second = diag_inv[section, 1]
    low_block = diag_low[section]
    first_all, second_all, low_all = (
        lax.all_gather(inv_first, "col", axis=1, tiled=True),
        lax.all_gather(inv_second, "col", axis=1, tiled=True),
        lax.all_gather(low_block, "col", axis=1, tiled=True),
    )
    half_rows = first_all.shape[0]
    first_at = jnp.minimum(offset, half_rows - own_rows)
    chosen = lax.dynamic_slice_in_dim(first_all, first_at, own_rows, 1)
    upper = jnp.concatenate([chosen, -mult(second_all, mult(low_all, chosen))], 0)
    second_at = jnp.clip(offset - half_rows, 0, half_rows - own_rows)
    picked = lax.dynamic_slice_in_dim(second_all, second_at, own_rows, 1)
    bottom = jnp.concatenate([jnp.zeros((half_rows, own_rows), f32), picked], 0)
    return jnp.where(offset < half_rows, upper, bottom)


def solve_step(diag_inv, diag_low, section, offset, own_rows, rows_block):
    inverse_cols = inverse_columns(diag_inv, diag_low, section, offset, own_rows)
    return lax.psum(mult(inverse_cols, rows_block), "row")


def general_shards(b_steps, b_trail, l_cross, l_trail, diag_inv, diag_low):
    own_rows = b_steps.shape[1]
    offset = lax.axis_index("row") * own_rows
    solved_first = solve_step(diag_inv, diag_low, 0, offset, own_rows, b_steps[0])
    next_rows = b_steps[1] - mult(lax.all_gather(l_cross, "col", axis=1, tiled=True), solved_first)
    trail = b_trail - mult(lax.all_gather(l_trail[0], "col", axis=1, tiled=True), solved_first)
    solved_second = solve_step(diag_inv, diag_low, 1, offset, own_rows, next_rows)
    trail = trail - mult(lax.all_gather(l_trail[1], "col", axis=1, tiled=True), solved_second)
    mine_first = lax.dynamic_slice_in_dim(solved_first, offset, own_rows, 0)
    mine_second = lax.dynamic_slice_in_dim(solved_second, offset, own_rows, 0)
    return (jnp.stack([mine_first, mine_second]), trail)


def halves(a):
    hi = a.astype(bf16)
    return hi, (a - hi.astype(f32)).astype(bf16)


def dot3(a, b):
    (ah, al), (bh, bl) = halves(a), halves(b)
    d = functools.partial(jnp.dot, preferred_element_type=f32)
    return d(ah, bh) + (d(ah, bl) + d(al, bh))


def solve_body(at, n_row, n_z, own_ref, parts, b_parts, mats, rhs):
    z, r, core = at
    width = own_ref.shape[-1]
    stripe = parts[0][0].shape[-2]
    for m in range(3):
        mats[m, :, pl.ds(pl.multiple_of(z * width, width), width)] = own_ref[0, m]
        for i in range(n_row):
            for q in range(2):
                row_at = pl.multiple_of(((r ^ i) * 2 + (core ^ q)) * stripe, stripe)
                for j in range(1, n_z):
                    lane_at = pl.multiple_of((z ^ j) * width, width)
                    mats[m, pl.ds(row_at, stripe), pl.ds(lane_at, width)] = parts[i][q][0, j - 1, m]
    block = b_parts[0].shape[0]
    for i in range(n_row):
        rhs[pl.ds(pl.multiple_of((r ^ i) * block, block), block), :] = b_parts[i][...]
    half = mats.shape[1]
    top = dot3(mats[0], rhs[:half])
    low = rhs[half:] - dot3(mats[2], top)
    return top, dot3(mats[1], low)


def first_kernel(n_row, n_z, at_ref, own_ref, *refs):
    parts = [[refs[2 * i + q] for q in range(2)] for i in range(n_row)]
    refs = refs[2 * n_row :]
    b_parts, refs = refs[:n_row], refs[n_row:]
    cross, refs = refs[: 2 * n_z], refs[2 * n_z :]
    b_next, x_ref, give_ref, next_ref, mats, rhs = refs
    at = z, r, core = at_ref[0], at_ref[1], at_ref[2]
    top, bottom = solve_body(at, n_row, n_z, own_ref, parts, b_parts, mats, rhs)
    half = top.shape[0]
    x_ref[:half] = top
    x_ref[half:] = bottom
    wide = cross[0].shape[1]
    total = b_next[...]
    for q in range(2):
        for j in range(n_z):
            k_at = pl.multiple_of(((z ^ j) * 2 + (core ^ q)) * wide, wide)
            total = total - dot3(cross[q * n_z + j][...], x_ref[pl.ds(k_at, wide), :])
    next_ref[...] = total
    for j in range(n_z):
        give_ref[j] = x_ref[pl.ds(pl.multiple_of((j * 2 + 1 - core) * wide, wide), wide), :]


def second_kernel(n_row, n_z, wide, at_ref, own_ref, *refs):
    parts = [[refs[2 * i + q] for q in range(2)] for i in range(n_row)]
    refs = refs[2 * n_row :]
    b_parts, refs = refs[:n_row], refs[n_row:]
    first_ref, x_ref, give_ref, steps_ref, mats, rhs = refs
    at = z, r, core = at_ref[0], at_ref[1], at_ref[2]
    top, bottom = solve_body(at, n_row, n_z, own_ref, parts, b_parts, mats, rhs)
    half = top.shape[0]
    x_ref[:half] = top
    x_ref[half:] = bottom
    for j in range(n_z):
        give_ref[j] = x_ref[pl.ds(pl.multiple_of((j * 2 + 1 - core) * wide, wide), wide), :]
    block = steps_ref.shape[1]
    mine = pl.ds(pl.multiple_of(r * block, block), block)
    steps_ref[0] = first_ref[mine, :]
    steps_ref[1] = x_ref[mine, :]


def trail_kernel(tags, at_ref, *refs):
    pieces, refs = refs[: len(tags)], refs[len(tags) :]
    x_refs, got_refs, acc_refs, outs = refs[:2], refs[2:4], refs[4:6], refs[6:]
    z, core = at_ref[0], at_ref[2]
    wide = pieces[0].shape[1]
    own, other = acc_refs[0][...], acc_refs[1][...]
    for (s, j), piece in zip(tags, pieces):
        k_at = pl.multiple_of(((z ^ j) * 2 + core) * wide, wide)
        left = piece[...]
        own = own - dot3(left, x_refs[s][pl.ds(k_at, wide), :])
        other = other - dot3(left, got_refs[s][z ^ j])
    outs[0][...] = own
    outs[1][...] = other


def vmem(n):
    return [pl.BlockSpec(memory_space=pltpu.VMEM)] * n


def smem():
    return pl.BlockSpec(memory_space=pltpu.SMEM)


def fast_shards(n_row, n_col, b_steps, b_trail, l_cross, l_trail, diag_inv, diag_low):
    n_z = n_col // 2
    r = lax.axis_index("row")
    c = lax.axis_index("col")
    z, core = c // 2, c % 2
    at = jnp.stack([z, r, core]).astype(jnp.int32)

    def swap(a):
        return lax.ppermute(a, "col", [(i, i ^ 1) for i in range(n_col)])

    def over_z(a, j):
        return lax.ppermute(a, "col", [(i, i ^ (2 * j)) for i in range(n_col)])

    def over_row(a, i):
        return lax.ppermute(a, "row", [(k, k ^ i) for k in range(n_row)])

    def far_z(a, second):
        middle = [(i, i ^ 6) for i in range(n_col) if (i // 2) % 4 in (1, 2)]
        onward = [(i, i ^ 2) for i in range(n_col) if (i // 2) % 4 in (1, 2)]
        return lax.ppermute(a, "col", middle), lax.ppermute(second, "col", onward)

    def gather_z(a):
        got = [a]
        for j in range(1, n_z):
            if j == 3:
                near, far = far_z(a, got[2])
                got.append(near + far)
            else:
                got.append(over_z(a, j))
        return got

    b_first = [b_steps[0]] + [over_row(b_steps[0], i) for i in range(1, n_row)]

    mats = jnp.concatenate([diag_inv, diag_low[:, None]], 1)
    theirs = swap(mats)
    chip = jnp.where(core == 0, jnp.concatenate([mats, theirs], 3), jnp.concatenate([theirs, mats], 3))
    n_stripe = 2 * n_row
    stripe = chip.shape[2] // n_stripe
    mine = lax.dynamic_slice_in_dim(chip, (r * 2 + core) * stripe, stripe, 2)
    others = jnp.stack(gather_z(mine)[1:], 1)
    by_row = [others] + [over_row(others, i) for i in range(1, n_row)]
    parts = []
    for a in by_row:
        parts += [a, swap(a)]

    cross = gather_z(l_cross)
    cross = cross + [swap(a) for a in cross]

    pieces, tags = [], []
    late, late_tags = [], []
    for s in range(2):
        got = [l_trail[s]]
        for j in range(1, n_z):
            if j == 3:
                near, far = far_z(l_trail[s], got[2])
                pieces.append(near)
                tags.append((s, j))
                late.append(far)
                late_tags.append((s, j))
            else:
                got.append(over_z(l_trail[s], j))
        pieces += got
        tags += [(s, j) for j in range(len(got))]

    half = chip.shape[2]
    nb, width = 2 * half, b_steps.shape[2]
    block, wide = b_steps.shape[1], l_cross.shape[1]
    own_spec = lambda s: pl.BlockSpec((1,) + chip.shape[1:], lambda i: (s, 0, 0, 0))
    part_spec = lambda s: pl.BlockSpec((1,) + others.shape[1:], lambda i: (s, 0, 0, 0, 0))
    full = lambda shape: pl.BlockSpec(shape, lambda i: (0,) * len(shape))
    scratch = [pltpu.VMEM((3, half, half), f32), pltpu.VMEM((nb, width), f32)]
    sds = lambda *shape: jax.ShapeDtypeStruct(shape, f32)
    x_first, give_first, next_own = pl.pallas_call(
        functools.partial(first_kernel, n_row, n_z),
        grid=(1,),
        in_specs=[smem(), own_spec(0)]
        + [part_spec(0)] * len(parts)
        + [full((block, width))] * n_row
        + [full(l_cross.shape)] * len(cross)
        + [full((block, width))],
        out_specs=[full((nb, width)), full((n_z, wide, width)), full((block, width))],
        out_shape=[sds(nb, width), sds(n_z, wide, width), sds(block, width)],
        scratch_shapes=scratch,
        name="first_step",
    )(at, chip, *parts, *b_first, *cross, b_steps[1])
    b_second = [next_own] + [over_row(next_own, i) for i in range(1, n_row)]
    x_second, give_second, x_steps = pl.pallas_call(
        functools.partial(second_kernel, n_row, n_z, wide),
        grid=(1,),
        in_specs=[smem(), own_spec(1)]
        + [part_spec(1)] * len(parts)
        + [full((block, width))] * n_row
        + [full((nb, width))],
        out_specs=[full((nb, width)), full((n_z, wide, width)), full((2, block, width))],
        out_shape=[sds(nb, width), sds(n_z, wide, width), sds(2, block, width)],
        scratch_shapes=scratch,
        name="second_step",
    )(at, chip, *parts, *b_second, x_first)
    got_first, got_second = swap(give_first), swap(give_second)

    rows = b_trail.shape[0]
    tile = rows // 4

    def trail(tags, pieces, own, other, name):
        tall = lambda w: pl.BlockSpec((tile, w), lambda i: (i, 0))
        return pl.pallas_call(
            functools.partial(trail_kernel, tags),
            grid=(rows // tile,),
            in_specs=[smem()]
            + [tall(wide)] * len(pieces)
            + [full((nb, width))] * 2
            + [full((n_z, wide, width))] * 2
            + [tall(width)] * 2,
            out_specs=[tall(width)] * 2,
            out_shape=[sds(rows, width)] * 2,
            name=name,
        )(at, *pieces, x_first, x_second, got_first, got_second, own, other)

    own, other = trail(tags, pieces, b_trail, jnp.zeros_like(b_trail), "trail_most")
    if late:
        own, other = trail(late_tags, late, own, other, "trail_rest")
    return x_steps, own + swap(other)


def shards(n_row, n_col, *args):
    b_steps, b_trail, l_cross, l_trail, diag_inv, diag_low = args
    n_z = n_col // 2
    half = diag_inv.shape[2]
    fits = (
        l_cross.shape[1] % LANES == 0
        and 2 * diag_inv.shape[3] % LANES == 0
        and b_steps.shape[2] % LANES == 0
        and half % (16 * n_row) == 0
        and b_trail.shape[0] % 32 == 0
        and n_row & (n_row - 1) == 0
        and n_col & (n_col - 1) == 0
        and n_col > 2
    )
    return fast_shards(n_row, n_col, *args) if fits else general_shards(*args)


def solution(mesh):
    placed = (
        P(None, "row", "col"),
        P("row", "col"),
        P("row", "col"),
        P(None, "row", "col"),
        P(None, None, None, "col"),
        P(None, None, "col"),
    )
    return jax.shard_map(
        functools.partial(shards, mesh.shape["row"], mesh.shape["col"]),
        mesh=mesh,
        in_specs=placed,
        out_specs=(P(None, "row", "col"), P("row", "col")),
        check_vma=False,
    )
```
